32 devices in a mesh: space: 8 (over y, x, core), level: 4 (over z).
Axes of the slice: x: 2, y: 2, z: 4, core: 2. Of those that a mesh axis runs over, the one named last changes fastest.
Arguments:
- fields: bfloat16 [4, 4096, 768], P('level', 'space'), may hold values from -16 to 16
- norm_vert: float32 [768], replicated, may hold values from 0.1 to 1.9
- query_vert: bfloat16 [768, 768], replicated, may hold values from -0.21875 to 0.21875
- keys_vert: bfloat16 [768, 768], replicated, may hold values from -0.21875 to 0.21875
- values_vert: bfloat16 [768, 768], replicated, may hold values from -0.21875 to 0.21875
- out_vert: bfloat16 [768, 768], replicated, may hold values from -0.21875 to 0.21875
- level_bias: float32 [12, 4, 4], replicated, may hold values from -3 to 250
- norm_patch: float32 [768], replicated, may hold values from 0.1 to 1.9
- query_patch: bfloat16 [768, 768], replicated, may hold values from -0.21875 to 0.21875
- keys_patch: bfloat16 [768, 768], replicated, may hold values from -0.21875 to 0.21875
- values_patch: bfloat16 [768, 768], replicated, may hold values from -0.21875 to 0.21875
- out_patch: bfloat16 [768, 768], replicated, may hold values from -0.21875 to 0.21875
- patch_bias: float32 [12, 2], replicated, may hold values from -3 to 250
- neighbours: int32 [16, 4], P('space'), may hold values from -1 to 15, as said below
- counts: int32 [16], P('space'), may hold values from 2 to 4, as said below
- cotangent: bfloat16 [4, 4096, 768], P('level', 'space'), may hold values from -0.046875 to 0.046875
Outputs:
- out_fields: bfloat16 [4, 4096, 768], P('level', 'space')
- grad_wo: float32 [768, 768], P('space')
The draws below stay inside these ranges and needn't reach their ends.
Inputs may be any that keep to these rules, and one draw needn't show every extreme that they name: `neighbours`: row p lists distinct patches, at most one from each device of space, held on devices at cycle distance 1 to 2 from the device of patch p (device s of space holds patches s * 2 to (s + 1) * 2 - 1); entries from counts[p] on are -1. `counts`: some patch has 4 neighbours in every draw.
All inputs are finite; a program needn't handle non-finite values.
Results may differ from the reference program's by a relative error of at most 0.025.
Values may be sent and summed in bfloat16 or wider, within the bound.
A program may use at most 128 MiB of HBM per device.

```python
import jax
import jax.numpy as jnp
from jax import lax

D = 768
H = 12
HD = 64
PATCH = 256
REACH = 2
PAT_DEV = 2
MAXN = 4
LEV = 4
PATCHES = 16
COLS = 4096
N_SPACE = 8


def draw_fields(key, part):
    noise_key = jax.random.fold_in(key, 0)
    sample = jax.random.normal(noise_key, (LEV, COLS, D), jnp.float32)
    return jnp.clip(sample, -16.0, 16.0).astype(jnp.bfloat16)


def draw_level_bias(key, part):
    noise_key = jax.random.fold_in(key, 0)
    sample = jnp.clip(jax.random.normal(noise_key, (H, LEV, LEV), jnp.float32), -3.0, 3.0)
    return sample


def draw_patch_bias(key, part):
    noise_key = jax.random.fold_in(jax.random.fold_in(key, 11), 0)
    sample = jnp.clip(jax.random.normal(noise_key, (H, 2), jnp.float32), -3.0, 3.0)
    return sample


def neighbour_tables(key):
    base_key = jax.random.fold_in(key, 29)
    order_key, count_key, within_key, full_key = jax.random.split(base_key, 4)
    orders = jax.vmap(lambda one_key: jax.random.permutation(one_key, 2 * REACH))(jax.random.split(order_key, PATCHES))
    signed = jnp.where(orders < REACH, orders + 1, REACH - 1 - orders)
    owners = jnp.arange(PATCHES, dtype=jnp.int32) // PAT_DEV
    far_owner = (owners[:, None] + signed) % N_SPACE
    within = jax.random.randint(within_key, (PATCHES, MAXN), 0, PAT_DEV)
    listed = far_owner * PAT_DEV + within
    tallies = jax.random.randint(count_key, (PATCHES,), 2, MAXN + 1)
    full_patch = jax.random.randint(full_key, (), 0, PATCHES)
    tallies = jnp.where(jnp.arange(PATCHES) == full_patch, MAXN, tallies)
    listed = jnp.where(jnp.arange(MAXN)[None, :] < tallies[:, None], listed, -1)
    return (listed.astype(jnp.int32), tallies.astype(jnp.int32))


def draw_neighbours(key, part):
    return neighbour_tables(key)[0]


def draw_counts(key, part):
    return neighbour_tables(key)[1]


def block_scale(key, dims, cuts, low, largest):
    level = 1.0
    for dim, blocks in cuts:
        steps = jax.random.uniform(jax.random.fold_in(jax.random.fold_in(key, 6), dim), (blocks,), jnp.float32, low / len(cuts), largest / len(cuts))
        level = level * jnp.repeat(jnp.exp(steps), dims[dim] // blocks).reshape((-1,) + (1,) * (len(dims) - 1 - dim))
    return level


def centred(own_key, dims, scale, bound, shards=(), kind=jnp.bfloat16):
    entries = jax.random.normal(own_key, dims, jnp.float32) * scale
    if len(shards) > 0:
        entries = block_scale(own_key, dims, shards, -0.22, 0.18) * entries
    return jnp.clip(entries, min=-bound, max=bound).astype(kind)


def setup_inputs(seed: int = 0) -> dict:
    streams_of = jax.random.split(jax.random.key(seed), 17)
    return {
        "fields": draw_fields(jax.random.fold_in(streams_of[16], 71), 0),
        "norm_vert": jnp.clip(1.0 + 0.18 * jax.random.normal(streams_of[1], (D,), jnp.float32), 0.1, 1.9),
        "query_vert": centred(streams_of[2], (D, D), D ** -0.5, 0.21875),
        "keys_vert": centred(streams_of[3], (D, D), D ** -0.5, 0.21875),
        "values_vert": centred(streams_of[4], (D, D), D ** -0.5, 0.21875),
        "out_vert": centred(streams_of[5], (D, D), D ** -0.5, 0.21875),
        "level_bias": draw_level_bias(jax.random.fold_in(streams_of[16], 71), 0),
        "norm_patch": jnp.clip(1.0 + 0.18 * jax.random.normal(streams_of[7], (D,), jnp.float32), 0.1, 1.9),
        "query_patch": centred(streams_of[8], (D, D), D ** -0.5, 0.21875),
        "keys_patch": centred(streams_of[9], (D, D), D ** -0.5, 0.21875),
        "values_patch": centred(streams_of[10], (D, D), D ** -0.5, 0.21875),
        "out_patch": centred(streams_of[11], (D, D), D ** -0.5, 0.21875),
        "patch_bias": draw_patch_bias(jax.random.fold_in(streams_of[16], 71), 0),
        "neighbours": draw_neighbours(jax.random.fold_in(streams_of[16], 71), 0),
        "counts": draw_counts(jax.random.fold_in(streams_of[16], 71), 0),
        "cotangent": centred(streams_of[15], (LEV, COLS, D), (LEV * COLS) ** -0.5, 0.046875, ((0, 4), (1, 8))),
    }


epsilon = 1e-06

def normalize(values, scaling):
    widened = values.astype(jnp.float32)
    mean_square = lax.optimization_barrier(jnp.mean(widened * widened, axis=-1, keepdims=True))
    return (widened * lax.rsqrt(mean_square + epsilon) * scaling).astype(jnp.bfloat16)

def project(inputs, weight):
    return jnp.dot(inputs, weight, preferred_element_type=jnp.float32).astype(jnp.bfloat16)

def vertical_mix(queries, keys_in, values_in, bias_table):
    level_count, columns, features = queries.shape
    query_heads = queries.astype(jnp.float32).reshape(level_count, columns, H, HD)
    key_heads = keys_in.astype(jnp.float32).reshape(keys_in.shape[0], columns, H, HD)
    value_heads = values_in.astype(jnp.float32).reshape(values_in.shape[0], columns, H, HD)
    scores = jnp.einsum('ichd,jchd->hijc', query_heads, key_heads) * HD ** (-0.5) + bias_table[:, :, :, None]
    weights = jax.nn.softmax(scores, axis=2).astype(jnp.bfloat16)
    mixture = jnp.einsum('hijc,jchd->ichd', weights.astype(jnp.float32), value_heads)
    return mixture.astype(jnp.bfloat16).reshape(level_count, columns, features)

def patch_mix(queries, own_keys, nearby, live_count, bias_table):
    features = queries.shape[-1]
    patch_len = own_keys.shape[0]
    keys_all = jnp.concatenate((own_keys[None], nearby), axis=0).reshape(-1, 2 * features)
    query_heads = queries.astype(jnp.float32).reshape(-1, H, HD)
    key_heads = keys_all[:, :features].astype(jnp.float32).reshape(-1, H, HD)
    value_heads = keys_all[:, features:].astype(jnp.float32).reshape(-1, H, HD)
    scores = jnp.einsum('qhd,khd->hqk', query_heads, key_heads) * HD ** (-0.5)
    block_bias = jnp.concatenate((bias_table[:, :1], jnp.broadcast_to(bias_table[:, 1:], (H, nearby.shape[0]))), axis=1)
    scores = scores + jnp.repeat(block_bias, patch_len, axis=1)[:, None, :]
    opened = jnp.repeat(jnp.arange(nearby.shape[0] + 1, dtype=jnp.int32) <= live_count, patch_len)
    scores = jnp.where(opened[None, None, :], scores, -jnp.inf)
    weights = jax.nn.softmax(scores, axis=-1).astype(jnp.bfloat16)
    mixture = jnp.einsum('hqk,khd->qhd', weights.astype(jnp.float32), value_heads)
    return mixture.astype(jnp.bfloat16).reshape(-1, features)

def reference(fields, norm_vert, query_vert, keys_vert, values_vert, out_vert, level_bias, norm_patch, query_patch, keys_patch, values_patch, out_patch, patch_bias, neighbours, counts, cotangent):
    normed = normalize(fields, norm_vert)
    attn_vert = vertical_mix(project(normed, query_vert), project(normed, keys_vert), project(normed, values_vert), level_bias)
    hidden = (fields.astype(jnp.float32) + jnp.dot(attn_vert, out_vert, preferred_element_type=jnp.float32)).astype(jnp.bfloat16)
    normed_patch = normalize(hidden, norm_patch)
    queries = project(normed_patch, query_patch).reshape(LEV, PATCHES, PATCH, D)
    key_values = jnp.concatenate((project(normed_patch, keys_patch), project(normed_patch, values_patch)), axis=-1).reshape(LEV, PATCHES, PATCH, 2 * D)

    def one_patch(patch_index):
        near_ids = jnp.maximum(neighbours[patch_index], 0).astype(jnp.int32)
        nearby = jnp.take(key_values, near_ids, axis=1)
        own_keys = key_values[:, patch_index]
        own_queries = queries[:, patch_index]
        return jax.vmap(patch_mix, in_axes=(0, 0, 0, None, None))(own_queries, own_keys, nearby, counts[patch_index], patch_bias)
    mixture = lax.map(one_patch, jnp.arange(PATCHES, dtype=jnp.int32))
    attn_patch = jnp.moveaxis(mixture, 0, 1).reshape(LEV, COLS, D)
    out_fields = (hidden.astype(jnp.float32) + jnp.dot(attn_patch, out_patch, preferred_element_type=jnp.float32)).astype(jnp.bfloat16)
    grad_wo = lax.dot_general(attn_patch.reshape(-1, D), cotangent.reshape(-1, D), (((0,), (0,)), ((), ())), preferred_element_type=jnp.float32)
    return (out_fields, grad_wo)
```

```python
import functools

import jax
import jax.numpy as jnp
from jax import lax
from jax.experimental import pallas as pl
from jax.experimental.pallas import tpu as pltpu
from jax.sharding import PartitionSpec as P

HD = 64
PATCH = 256
REACH = 2
LANES = 128
VMEM_LIMIT = 58 * 1024 * 1024

epsilon = 1e-06
OFFSETS = [stride for stride in range(1, REACH + 1)] + [-stride for stride in range(1, REACH + 1)]


def passed_along(value, axis, steps):
    count = lax.axis_size(axis)
    pairs = [(source, (source + steps) % count) for source in range(count)]
    return lax.ppermute(value, axis, pairs)


def normalized(widened, scaling):
    mean_square = jnp.mean(widened * widened, axis=-1, keepdims=True)
    return (widened * lax.rsqrt(mean_square + epsilon) * scaling).astype(jnp.bfloat16)


def project(inputs, weight):
    return jnp.dot(inputs, weight, preferred_element_type=jnp.float32).astype(jnp.bfloat16)


def vertical_kernel(x_ref, gain_ref, wq_ref, wk_ref, wv_ref, wo_ref, bias_ref, hidden_ref, attn_ref):
    levels, columns, features = x_ref.shape
    tokens = levels * columns
    x = x_ref[...].reshape(tokens, features).astype(jnp.float32)
    normed = normalized(x, gain_ref[...])
    queries = project(normed, wq_ref[...]).astype(jnp.float32)
    keys = project(normed, wk_ref[...]).astype(jnp.float32)
    values = project(normed, wv_ref[...]).astype(jnp.float32)
    head_of = lax.broadcasted_iota(jnp.int32, (features, LANES), 0) // HD
    gather_heads = (head_of == lax.broadcasted_iota(jnp.int32, (features, LANES), 1)).astype(jnp.bfloat16)
    head_to = lax.broadcasted_iota(jnp.int32, (LANES, features), 1) // HD
    spread_heads = (head_to == lax.broadcasted_iota(jnp.int32, (LANES, features), 0)).astype(jnp.bfloat16)
    for i in range(levels):
        query = queries[i * columns : (i + 1) * columns]
        products = jnp.concatenate(
            [(query * keys[j * columns : (j + 1) * columns]).astype(jnp.bfloat16) for j in range(levels)], axis=0
        )
        summed = jnp.dot(products, gather_heads, preferred_element_type=jnp.float32) * HD ** (-0.5)
        scores = [
            summed[j * columns : (j + 1) * columns] + bias_ref[i * levels + j : i * levels + j + 1, :]
            for j in range(levels)
        ]
        top = functools.reduce(jnp.maximum, scores)
        raised = [jnp.exp(score - top) for score in scores]
        inverse = 1.0 / functools.reduce(jnp.add, raised)
        weights = jnp.concatenate([(each * inverse).astype(jnp.bfloat16) for each in raised], axis=0)
        spread = jnp.dot(weights, spread_heads, preferred_element_type=jnp.float32)
        mixed = functools.reduce(
            jnp.add,
            [
                spread[j * columns : (j + 1) * columns] * values[j * columns : (j + 1) * columns]
                for j in range(levels)
            ],
        )
        attn_ref[i * columns : (i + 1) * columns, :] = mixed.astype(jnp.bfloat16)
    hidden = x + jnp.dot(attn_ref[...], wo_ref[...], preferred_element_type=jnp.float32)
    hidden_ref[...] = hidden.astype(jnp.bfloat16).reshape(levels, columns, features)


def vertical(merged, gain, wq, wk, wv, wo, bias_rows):
    levels, columns, features = merged.shape
    vmem = pl.BlockSpec(memory_space=pltpu.VMEM)
    return pl.pallas_call(
        vertical_kernel,
        out_shape=jax.ShapeDtypeStruct(merged.shape, jnp.bfloat16),
        in_specs=[vmem] * 7,
        out_specs=vmem,
        scratch_shapes=[pltpu.VMEM((levels * columns, features), jnp.bfloat16)],
        compiler_params=pltpu.CompilerParams(vmem_limit_bytes=VMEM_LIMIT),
        name="vertical",
    )(merged, gain, wq, wk, wv, wo, bias_rows)


def choices(nb_ref, count_ref, patch, offset, cycle, per_device):
    source = lax.rem(lax.axis_index("space") + cycle - offset, cycle)
    live = jnp.int32(0)
    within = jnp.int32(0)
    for m in range(nb_ref.shape[1]):
        listed = jnp.maximum(nb_ref[patch, m], 0)
        hit = jnp.logical_and(m < count_ref[patch], lax.div(listed, per_device) == source)
        live = jnp.where(hit, 1, live)
        within = jnp.where(hit, lax.rem(listed, per_device), within)
    return live, within


def attend(q_ref, k_ref, v_ref, attn_ref, pb_ref, nb_ref, count_ref, cycle):
    tokens, features = q_ref.shape
    per_device = tokens // PATCH
    far = len(OFFSETS) * per_device
    low = lax.broadcasted_iota(jnp.int32, (1, LANES), 1) < HD
    for patch in range(per_device):
        rows = pl.ds(patch * PATCH, PATCH)
        picked = [choices(nb_ref, count_ref, patch, offset, cycle, per_device) for offset in OFFSETS]
        blocks = [far + patch] + [o * per_device + within for o, (_, within) in enumerate(picked)]

        def pair(step, carry):
            lanes = pl.ds(pl.multiple_of(step * LANES, LANES), LANES)
            query = q_ref[rows, lanes]
            results = []
            for parity in range(2):
                head = step * 2 + parity
                mine = low if parity == 0 else jnp.logical_not(low)
                masked = jnp.where(mine, query, jnp.zeros_like(query))
                scores = [
                    lax.dot_general(
                        masked, k_ref[block, :, lanes], (((1,), (1,)), ((), ())), preferred_element_type=jnp.float32
                    )
                    for block in blocks
                ]
                adds = [pb_ref[head, 0]] + [
                    jnp.where(live > 0, pb_ref[head, 1], jnp.float32(-1e30)) for live, _ in picked
                ]
                top = functools.reduce(
                    jnp.maximum, [jnp.max(s, axis=-1, keepdims=True) + a for s, a in zip(scores, adds)]
                )
                raised = [jnp.exp(s + (a - top)) for s, a in zip(scores, adds)]
                total = functools.reduce(jnp.add, [jnp.sum(r, axis=-1, keepdims=True) for r in raised])
                mixed = functools.reduce(
                    jnp.add,
                    [
                        jnp.dot(r.astype(jnp.bfloat16), v_ref[block, :, lanes], preferred_element_type=jnp.float32)
                        for r, block in zip(raised, blocks)
                    ],
                )
                results.append(mixed / total)
            attn_ref[rows, lanes] = jnp.where(low, results[0], results[1]).astype(jnp.bfloat16)
            return carry

        lax.fori_loop(0, features // LANES, pair, 0)


def patch_kernel(cycle, xo_ref, xf_ref, hid_ref, cot_ref, wq_ref, wk_ref, wv_ref, wo_ref, pb_ref, nb_ref, count_ref,
                 out_ref, grad_ref, q_ref, k_ref, v_ref, attn_ref):
    tokens, features = xo_ref.shape
    per_device = tokens // PATCH
    far = len(OFFSETS) * per_device
    own = xo_ref[...]
    q_ref[...] = (jnp.dot(own, wq_ref[...], preferred_element_type=jnp.float32).astype(jnp.bfloat16)
                  * jnp.bfloat16(HD ** (-0.5)))
    k_ref[far:] = project(own, wk_ref[...]).reshape(per_device, PATCH, features)
    v_ref[far:] = project(own, wv_ref[...]).reshape(per_device, PATCH, features)

    def distant(step, carry):
        block = xf_ref[step]
        k_ref[step] = project(block, wk_ref[...])
        v_ref[step] = project(block, wv_ref[...])
        return carry

    lax.fori_loop(0, far, distant, 0)
    attend(q_ref, k_ref, v_ref, attn_ref, pb_ref, nb_ref, count_ref, cycle)
    attn = attn_ref[...]
    grad_ref[...] = lax.dot_general(
        attn, cot_ref[...], (((0,), (0,)), ((), ())), preferred_element_type=jnp.float32
    ).astype(jnp.bfloat16)
    out_ref[...] = (
        hid_ref[...].astype(jnp.float32) + jnp.dot(attn, wo_ref[...], preferred_element_type=jnp.float32)
    ).astype(jnp.bfloat16)


def patch_stage(xo, xf, hidden, cot, wq, wk, wv, wo, pb, nb, counts):
    tokens, features = xo.shape
    blocks = (len(OFFSETS) + 1) * (tokens // PATCH)
    vmem = pl.BlockSpec(memory_space=pltpu.VMEM)
    smem = pl.BlockSpec(memory_space=pltpu.SMEM)
    return pl.pallas_call(
        functools.partial(patch_kernel, lax.axis_size("space")),
        out_shape=(
            jax.ShapeDtypeStruct((tokens, features), jnp.bfloat16),
            jax.ShapeDtypeStruct((features, features), jnp.bfloat16),
        ),
        in_specs=[vmem] * 8 + [smem] * 3,
        out_specs=(vmem, vmem),
        scratch_shapes=[
            pltpu.VMEM((tokens, features), jnp.bfloat16),
            pltpu.VMEM((blocks, PATCH, features), jnp.bfloat16),
            pltpu.VMEM((blocks, PATCH, features), jnp.bfloat16),
            pltpu.VMEM((tokens, features), jnp.bfloat16),
        ],
        compiler_params=pltpu.CompilerParams(vmem_limit_bytes=VMEM_LIMIT),
        name="patch_stage",
    )(xo, xf, hidden, cot, wq, wk, wv, wo, pb, nb, counts)


def body(fields, norm_vert, query_vert, keys_vert, values_vert, out_vert, level_bias, norm_patch, query_patch,
         keys_patch, values_patch, out_patch, patch_bias, neighbours, counts, cotangent):
    _, columns, features = fields.shape
    groups = lax.axis_size("level")
    heads = level_bias.shape[0]
    bias_rows = jnp.pad(
        jnp.transpose(level_bias, (1, 2, 0)).reshape(groups * groups, heads), ((0, 0), (0, LANES - heads))
    )
    split = fields.reshape(groups, columns // groups, features)
    merged = lax.all_to_all(split, "level", split_axis=0, concat_axis=0, tiled=True)
    mixed = vertical(merged, norm_vert[None], query_vert, keys_vert, values_vert, out_vert, bias_rows)
    hidden = lax.all_to_all(mixed, "level", split_axis=0, concat_axis=0, tiled=True).reshape(columns, features)
    normed = normalized(hidden.astype(jnp.float32), norm_patch)
    arrived = jnp.concatenate([passed_along(normed, "space", offset)[None] for offset in OFFSETS])
    out, grad = patch_stage(normed, arrived.reshape(-1, PATCH, features), hidden, cotangent[0], query_patch,
                            keys_patch, values_patch, out_patch, patch_bias, neighbours, counts)
    shares = lax.psum_scatter(grad, "space", scatter_dimension=0, tiled=True)
    grad_wo = lax.psum(shares, "level").astype(jnp.float32)
    return (out[None], grad_wo)


def solution(mesh):
    split = P("level", "space", None)
    return jax.shard_map(
        body,
        mesh=mesh,
        in_specs=(split,) + (P(),) * 12 + (P("space", None), P("space"), split),
        out_specs=(split, P("space", None)),
        check_vma=False,
    )
```

```python
import functools

import jax
import jax.numpy as jnp
from jax import lax
from jax.experimental import pallas as pl
from jax.experimental.pallas import tpu as pltpu
from jax.sharding import PartitionSpec as P

HD = 64
PATCH = 256
LANES = 128
VMEM_LIMIT = 58 * 1024 * 1024

epsilon = 1e-06


def normalized(widened, scaling):
    mean_square = jnp.mean(widened * widened, axis=-1, keepdims=True)
    return (widened * lax.rsqrt(mean_square + epsilon) * scaling).astype(jnp.bfloat16)


def project(inputs, weight):
    return jnp.dot(inputs, weight, preferred_element_type=jnp.float32).astype(jnp.bfloat16)


def vertical(x, gain, wq, wk, wv, wo, bias_rows, attn_ref):
    levels, columns, features = x.shape
    tokens = levels * columns
    x = x.reshape(tokens, features).astype(jnp.float32)
    normed = normalized(x, gain)
    queries = project(normed, wq).astype(jnp.float32)
    keys = project(normed, wk).astype(jnp.float32)
    values = project(normed, wv).astype(jnp.float32)
    head_of = lax.broadcasted_iota(jnp.int32, (features, LANES), 0) // HD
    gather_heads = (head_of == lax.broadcasted_iota(jnp.int32, (features, LANES), 1)).astype(jnp.bfloat16)
    head_to = lax.broadcasted_iota(jnp.int32, (LANES, features), 1) // HD
    spread_heads = (head_to == lax.broadcasted_iota(jnp.int32, (LANES, features), 0)).astype(jnp.bfloat16)
    for i in range(levels):
        query = queries[i * columns : (i + 1) * columns]
        products = jnp.concatenate(
            [(query * keys[j * columns : (j + 1) * columns]).astype(jnp.bfloat16) for j in range(levels)], axis=0
        )
        summed = jnp.dot(products, gather_heads, preferred_element_type=jnp.float32) * HD ** (-0.5)
        scores = [
            summed[j * columns : (j + 1) * columns] + bias_rows[i * levels + j]
            for j in range(levels)
        ]
        top = functools.reduce(jnp.maximum, scores)
        raised = [jnp.exp(score - top) for score in scores]
        inverse = 1.0 / functools.reduce(jnp.add, raised)
        weights = jnp.concatenate([(each * inverse).astype(jnp.bfloat16) for each in raised], axis=0)
        spread = jnp.dot(weights, spread_heads, preferred_element_type=jnp.float32)
        mixed = functools.reduce(
            jnp.add,
            [
                spread[j * columns : (j + 1) * columns] * values[j * columns : (j + 1) * columns]
                for j in range(levels)
            ],
        )
        attn_ref[i * columns : (i + 1) * columns, :] = mixed.astype(jnp.bfloat16)
    hidden = x + jnp.dot(attn_ref[...], wo, preferred_element_type=jnp.float32)
    return hidden.astype(jnp.bfloat16).reshape(levels, columns, features)


def choices(nb_ref, count_ref, patch, source, per_device):
    live = jnp.int32(0)
    within = jnp.int32(0)
    for m in range(nb_ref.shape[1]):
        listed = jnp.maximum(nb_ref[patch, m], 0)
        hit = jnp.logical_and(m < count_ref[patch], lax.div(listed, per_device) == source)
        live = jnp.where(hit, 1, live)
        within = jnp.where(hit, lax.rem(listed, per_device), within)
    return live, within


def attend(q_ref, k_ref, v_ref, attn_ref, pb_ref, nb_ref, count_ref, sources):
    tokens, features = q_ref.shape
    per_device = tokens // PATCH
    far = len(sources) * per_device
    low = lax.broadcasted_iota(jnp.int32, (1, LANES), 1) < HD
    for patch in range(per_device):
        rows = pl.ds(patch * PATCH, PATCH)
        picked = [choices(nb_ref, count_ref, patch, source, per_device) for source in sources]
        blocks = [far + patch] + [o * per_device + within for o, (_, within) in enumerate(picked)]

        def pair(step, carry):
            lanes = pl.ds(pl.multiple_of(step * LANES, LANES), LANES)
            query = q_ref[rows, lanes]
            results = []
            for parity in range(2):
                head = step * 2 + parity
                mine = low if parity == 0 else jnp.logical_not(low)
                masked = jnp.where(mine, query, jnp.zeros_like(query))
                scores = [
                    lax.dot_general(
                        masked, k_ref[block, :, lanes], (((1,), (1,)), ((), ())), preferred_element_type=jnp.float32
                    )
                    for block in blocks
                ]
                adds = [pb_ref[head, 0]] + [
                    jnp.where(live > 0, pb_ref[head, 1], jnp.float32(-1e30)) for live, _ in picked
                ]
                top = functools.reduce(
                    jnp.maximum, [jnp.max(s, axis=-1, keepdims=True) + a for s, a in zip(scores, adds)]
                )
                raised = [jnp.exp(s + (a - top)) for s, a in zip(scores, adds)]
                total = functools.reduce(jnp.add, [jnp.sum(r, axis=-1, keepdims=True) for r in raised])
                mixed = functools.reduce(
                    jnp.add,
                    [
                        jnp.dot(r.astype(jnp.bfloat16), v_ref[block, :, lanes], preferred_element_type=jnp.float32)
                        for r, block in zip(raised, blocks)
                    ],
                )
                results.append(mixed / total)
            attn_ref[rows, lanes] = jnp.where(low, results[0], results[1]).astype(jnp.bfloat16)
            return carry

        lax.fori_loop(0, features // LANES, pair, 0)


def remote(src, dst, send, recv, device):
    return pltpu.make_async_remote_copy(
        src_ref=src, dst_ref=dst, send_sem=send, recv_sem=recv, device_id=device,
        device_id_type=pl.DeviceIdType.MESH,
    )


def whole_kernel(cycle, levels, x_ref, nv_ref, np_ref, wqv_hbm, wkv_hbm, wvv_hbm, wov_hbm, wqp_hbm, wkp_hbm, wvp_hbm,
                 wop_hbm, cot_hbm, lb_ref, pb_ref, nb_ref, count_ref, out_ref, grad_ref, weight_ref, cot_ref, in_ref,
                 hsend_ref, hid_ref, attn_ref, own_ref, far_ref, q_ref, k_ref, v_ref, gsend_ref, grecv_ref, lsend_ref,
                 lrecv_ref, final_ref, load_sem, in_send, in_recv, back_send, back_recv, halo_send, halo_recv,
                 share_send, share_recv, part_send, part_recv, full_send, full_recv):
    chunks, _, columns, features = x_ref.shape
    place = lax.axis_index("space")
    level = lax.axis_index("level")
    weights_hbm = (wqv_hbm, wkv_hbm, wvv_hbm, wov_hbm, wqp_hbm, wkp_hbm, wvp_hbm, wop_hbm)
    loads = [pltpu.make_async_copy(w, weight_ref.at[i], load_sem.at[i]) for i, w in enumerate(weights_hbm)]
    loads.append(pltpu.make_async_copy(cot_hbm, cot_ref, load_sem.at[len(weights_hbm)]))
    for load in loads:
        load.start()

    barrier = pltpu.get_barrier_semaphore()
    peers = [lax.rem(level + k, levels) for k in range(1, levels)]
    around = [lax.rem(place + k, cycle) for k in range(1, cycle)]
    for peer in peers:
        pl.semaphore_signal(barrier, inc=1, device_id={"level": peer}, device_id_type=pl.DeviceIdType.MESH)
    for peer in around:
        pl.semaphore_signal(barrier, inc=1, device_id={"space": peer}, device_id_type=pl.DeviceIdType.MESH)
    pl.semaphore_wait(barrier, levels - 1 + cycle - 1)

    inward = []
    for c in range(chunks):
        steps = []
        for k, peer in enumerate(peers):
            steps.append(remote(x_ref.at[c, peer], in_ref.at[c, level], in_send.at[c, k], in_recv.at[c, k],
                                {"level": peer}))
            steps[-1].start()
        in_ref[c, level] = x_ref[c, level]
        inward.append(steps)

    lane = lax.broadcasted_iota(jnp.int32, (1, LANES), 1)
    bias_rows = []
    for i in range(levels):
        for j in range(levels):
            row = jnp.zeros((1, LANES), jnp.float32)
            for h in range(lb_ref.shape[0]):
                row = jnp.where(lane == h, lb_ref[h, i, j], row)
            bias_rows.append(row)
    for load in loads[:4]:
        load.wait()

    back = []
    for c in range(chunks):
        for step in inward[c]:
            step.wait_recv()
        hsend_ref[c] = vertical(in_ref[c], nv_ref[...], weight_ref[0], weight_ref[1], weight_ref[2], weight_ref[3],
                                bias_rows, attn_ref.at[pl.ds(0, PATCH)])
        steps = []
        for k, peer in enumerate(peers):
            steps.append(remote(hsend_ref.at[c, peer], hid_ref.at[c, level], back_send.at[c, k], back_recv.at[c, k],
                                {"level": peer}))
            steps[-1].start()
        hid_ref[c, level] = hsend_ref[c, level]
        back.append(steps)
    for load in loads[4:]:
        load.wait()

    toward = lax.rem(place, 2) * 2 - 1
    sources = [lax.rem(place + step * toward + 2 * cycle, cycle) for step in (1, 2, -1, -2)]
    partner = sources[2]
    far = len(sources) * chunks
    scale = jnp.bfloat16(HD ** (-0.5))
    halo = []
    for c in range(chunks):
        for step in back[c]:
            step.wait_recv()
        normed = normalized(hid_ref[c].reshape(levels * columns, features).astype(jnp.float32), np_ref[...])
        own_ref[c] = normed
        steps = []
        for slot, target in ((0, sources[0]), (1, sources[3]), (2, partner)):
            steps.append(remote(own_ref.at[c], far_ref.at[slot * chunks + c], halo_send.at[c, slot],
                                halo_recv.at[c, slot], {"space": target}))
            steps[-1].start()
        halo.append(steps)
        q_ref[pl.ds(c * PATCH, PATCH), :] = project(normed, weight_ref[4]) * scale
        k_ref[far + c] = project(normed, weight_ref[5])
        v_ref[far + c] = project(normed, weight_ref[6])
    def distant(block):
        k_ref[block] = project(far_ref[block], weight_ref[5])
        v_ref[block] = project(far_ref[block], weight_ref[6])

    for c in range(chunks):
        halo[c][2].wait_recv()
        distant(2 * chunks + c)
        halo[c][0].wait_recv()
        passed = remote(far_ref.at[c], far_ref.at[3 * chunks + c], halo_send.at[c, 3], halo_recv.at[c, 3],
                        {"space": partner})
        passed.start()
        halo[c].append(passed)
        distant(c)
        halo[c][1].wait_recv()
        distant(chunks + c)
    for c in range(chunks):
        halo[c][3].wait_recv()
        distant(3 * chunks + c)

    attend(q_ref, k_ref, v_ref, attn_ref, pb_ref, nb_ref, count_ref, sources)

    share = features // cycle
    total = lax.dot_general(attn_ref[...], cot_ref[...], (((0,), (0,)), ((), ())), preferred_element_type=jnp.float32)
    for d in range(cycle):
        gsend_ref[d] = total[d * share : (d + 1) * share].astype(jnp.bfloat16)
    shares = []
    for k, peer in enumerate(around):
        shares.append(remote(gsend_ref.at[peer], grecv_ref.at[k], share_send.at[k], share_recv.at[k],
                             {"space": peer}))
        shares[-1].start()
    out_ref[...] = (
        hid_ref[...].reshape(chunks * PATCH, features).astype(jnp.float32)
        + jnp.dot(attn_ref[...], weight_ref[7], preferred_element_type=jnp.float32)
    ).astype(jnp.bfloat16)
    gathered = gsend_ref[place].astype(jnp.float32)
    for k, step in enumerate(shares):
        step.wait_recv()
        gathered = gathered + grecv_ref[k].astype(jnp.float32)
    piece = share // levels
    for i in range(levels):
        lsend_ref[i] = gathered[i * piece : (i + 1) * piece].astype(jnp.bfloat16)
    parts = []
    for k, peer in enumerate(peers):
        parts.append(remote(lsend_ref.at[peer], lrecv_ref.at[k], part_send.at[k], part_recv.at[k], {"level": peer}))
        parts[-1].start()
    gathered = lsend_ref[level].astype(jnp.float32)
    for k, step in enumerate(parts):
        step.wait_recv()
        gathered = gathered + lrecv_ref[k].astype(jnp.float32)
    final_ref[level] = gathered.astype(jnp.bfloat16)
    fulls = []
    for k, peer in enumerate(peers):
        fulls.append(remote(final_ref.at[level], final_ref.at[level], full_send.at[k], full_recv.at[k],
                            {"level": peer}))
        fulls[-1].start()
    for step in fulls:
        step.wait_recv()
    for i in range(levels):
        grad_ref[i * piece : (i + 1) * piece, :] = final_ref[i].astype(jnp.float32)
    for steps in inward + back + halo + [shares, parts, fulls]:
        for step in steps:
            step.wait_send()


def body(fields, norm_vert, query_vert, keys_vert, values_vert, out_vert, level_bias, norm_patch, query_patch,
         keys_patch, values_patch, out_patch, patch_bias, neighbours, counts, cotangent):
    _, tokens, features = fields.shape
    levels = lax.axis_size("level")
    cycle = lax.axis_size("space")
    chunks = tokens // PATCH
    columns = PATCH // levels
    share = features // cycle
    x = fields.reshape(chunks, levels, columns, features)
    vmem = pl.BlockSpec(memory_space=pltpu.VMEM)
    smem = pl.BlockSpec(memory_space=pltpu.SMEM)
    hbm = pl.BlockSpec(memory_space=pl.ANY)
    narrow = lambda *shape: pltpu.VMEM(shape, jnp.bfloat16)
    dma = lambda *shape: pltpu.SemaphoreType.DMA(shape)
    blocks = 5 * chunks
    out, grad = pl.pallas_call(
        functools.partial(whole_kernel, cycle, levels),
        out_shape=(
            jax.ShapeDtypeStruct((tokens, features), jnp.bfloat16),
            jax.ShapeDtypeStruct((share, features), jnp.float32),
        ),
        in_specs=[vmem] * 3 + [hbm] * 9 + [smem] * 4,
        out_specs=(vmem, vmem),
        scratch_shapes=[
            narrow(8, features, features),
            narrow(tokens, features),
            narrow(chunks, levels, columns, features),
            narrow(chunks, levels, columns, features),
            narrow(chunks, levels, columns, features),
            narrow(tokens, features),
            narrow(chunks, PATCH, features),
            narrow(4 * chunks, PATCH, features),
            narrow(tokens, features),
            narrow(blocks, PATCH, features),
            narrow(blocks, PATCH, features),
            narrow(cycle, share, features),
            narrow(cycle - 1, share, features),
            narrow(levels, share // levels, features),
            narrow(levels - 1, share // levels, features),
            narrow(levels, share // levels, features),
            dma(9),
            dma(chunks, levels - 1),
            dma(chunks, levels - 1),
            dma(chunks, levels - 1),
            dma(chunks, levels - 1),
            dma(chunks, 4),
            dma(chunks, 4),
            dma(cycle - 1),
            dma(cycle - 1),
            dma(levels - 1),
            dma(levels - 1),
            dma(levels - 1),
            dma(levels - 1),
        ],
        compiler_params=pltpu.CompilerParams(
            collective_id=0, has_side_effects=True, vmem_limit_bytes=VMEM_LIMIT
        ),
        name="whole_block",
    )(x, norm_vert[None], norm_patch[None], query_vert, keys_vert, values_vert, out_vert, query_patch, keys_patch,
      values_patch, out_patch, cotangent[0], level_bias, patch_bias, neighbours, counts)
    return (out[None], grad)


def solution(mesh):
    split = P("level", "space", None)
    return jax.shard_map(
        body,
        mesh=mesh,
        in_specs=(split,) + (P(),) * 12 + (P("space", None), P("space"), split),
        out_specs=(split, P("space", None)),
        check_vma=False,
    )
```

```python
import functools
import math

import jax
import jax.numpy as jnp
from jax import lax
from jax.experimental import pallas as pl
from jax.experimental.pallas import tpu as pltpu
from jax.sharding import PartitionSpec as P

HD = 64
PATCH = 256
LANES = 128
SPLIT = 2
VMEM_LIMIT = 58 * 1024 * 1024

epsilon = 1e-06


def normalized(widened, scaling):
    mean_square = jnp.mean(widened * widened, axis=-1, keepdims=True)
    return (widened * lax.rsqrt(mean_square + epsilon) * scaling).astype(jnp.bfloat16)


def project(inputs, weight):
    return jnp.dot(inputs, weight, preferred_element_type=jnp.float32).astype(jnp.bfloat16)


def vertical(x, gain, wq, wk, wv, wo, bias_rows, attn_ref):
    levels, columns, features = x.shape
    tokens = levels * columns
    x = x.reshape(tokens, features).astype(jnp.float32)
    normed = normalized(x, gain)
    queries = project(normed, wq).astype(jnp.float32)
    keys = project(normed, wk).astype(jnp.float32)
    values = project(normed, wv).astype(jnp.float32)
    head_of = lax.broadcasted_iota(jnp.int32, (features, LANES), 0) // HD
    gather_heads = (head_of == lax.broadcasted_iota(jnp.int32, (features, LANES), 1)).astype(jnp.bfloat16)
    head_to = lax.broadcasted_iota(jnp.int32, (LANES, features), 1) // HD
    spread_heads = (head_to == lax.broadcasted_iota(jnp.int32, (LANES, features), 0)).astype(jnp.bfloat16)
    for i in range(levels):
        query = queries[i * columns : (i + 1) * columns]
        products = jnp.concatenate(
            [(query * keys[j * columns : (j + 1) * columns]).astype(jnp.bfloat16) for j in range(levels)], axis=0
        )
        summed = jnp.dot(products, gather_heads, preferred_element_type=jnp.float32) * HD ** (-0.5)
        scores = [
            summed[j * columns : (j + 1) * columns] + bias_rows[i * levels + j]
            for j in range(levels)
        ]
        top = functools.reduce(jnp.maximum, scores)
        raised = [jnp.exp(score - top) for score in scores]
        inverse = 1.0 / functools.reduce(jnp.add, raised)
        weights = jnp.concatenate([(each * inverse).astype(jnp.bfloat16) for each in raised], axis=0)
        spread = jnp.dot(weights, spread_heads, preferred_element_type=jnp.float32)
        mixed = functools.reduce(
            jnp.add,
            [
                spread[j * columns : (j + 1) * columns] * values[j * columns : (j + 1) * columns]
                for j in range(levels)
            ],
        )
        attn_ref[i * columns : (i + 1) * columns, :] = mixed.astype(jnp.bfloat16)
    hidden = x + jnp.dot(attn_ref[...], wo, preferred_element_type=jnp.float32)
    return hidden.astype(jnp.bfloat16).reshape(levels, columns, features)


def choices(nb_ref, count_ref, patch, source, per_device):
    live = jnp.int32(0)
    within = jnp.int32(0)
    for m in range(nb_ref.shape[1]):
        listed = jnp.maximum(nb_ref[patch, m], 0)
        hit = jnp.logical_and(m < count_ref[patch], lax.div(listed, per_device) == source)
        live = jnp.where(hit, 1, live)
        within = jnp.where(hit, lax.rem(listed, per_device), within)
    return live, within


def attend(step, q_ref, k_ref, v_ref, attn_ref, pb_ref, tables, far):
    low = lax.broadcasted_iota(jnp.int32, (1, LANES), 1) < HD
    lanes = pl.ds(pl.multiple_of(step * LANES, LANES), LANES)
    for patch, picked in enumerate(tables):
        rows = pl.ds(patch * PATCH, PATCH)
        blocks = [far + patch] + [o * len(tables) + within for o, (_, within) in enumerate(picked)]
        query = q_ref[rows, lanes]
        results = []
        for parity in range(2):
            head = step * 2 + parity
            mine = low if parity == 0 else jnp.logical_not(low)
            masked = jnp.where(mine, query, jnp.zeros_like(query))
            scores = [
                lax.dot_general(
                    masked, k_ref[block, :, lanes], (((1,), (1,)), ((), ())), preferred_element_type=jnp.float32
                )
                for block in blocks
            ]
            adds = [pb_ref[0, head]] + [
                jnp.where(live > 0, pb_ref[1, head], jnp.float32(-1e30)) for live, _ in picked
            ]
            top = functools.reduce(
                jnp.maximum, [jnp.max(s, axis=-1, keepdims=True) + a for s, a in zip(scores, adds)]
            )
            raised = [jnp.exp(s + (a - top)) for s, a in zip(scores, adds)]
            total = functools.reduce(jnp.add, [jnp.sum(r, axis=-1, keepdims=True) for r in raised])
            mixed = functools.reduce(
                jnp.add,
                [
                    jnp.dot(r.astype(jnp.bfloat16), v_ref[block, :, lanes], preferred_element_type=jnp.float32)
                    for r, block in zip(raised, blocks)
                ],
            )
            results.append(mixed / total)
        attn_ref[rows, lanes] = jnp.where(low, results[0], results[1]).astype(jnp.bfloat16)


def remote(src, dst, send, recv, device):
    return pltpu.make_async_remote_copy(
        src_ref=src, dst_ref=dst, send_sem=send, recv_sem=recv, device_id=device,
        device_id_type=pl.DeviceIdType.MESH,
    )


def whole_kernel(cycle, levels, x_ref, nv_ref, np_ref, wqv_hbm, wkv_hbm, wvv_hbm, wov_hbm, wqp_hbm, wkp_hbm, wvp_hbm,
                 wop_hbm, cot_hbm, lb_ref, pb_ref, nb_ref, count_ref, out_ref, grad_ref, weight_ref, cot_ref, in_ref,
                 hsend_ref, hid_ref, attn_ref, own_ref, far_ref, q_ref, k_ref, v_ref, gsend_ref, grecv_ref, lsend_ref,
                 lrecv_ref, final_ref, load_sem, in_send, in_recv, back_send, back_recv, halo_send, halo_recv,
                 share_send, share_recv, part_send, part_recv, full_send, full_recv):
    chunks, _, columns, features = x_ref.shape
    place = lax.axis_index("space")
    level = lax.axis_index("level")
    weights_hbm = (wqv_hbm, wkv_hbm, wvv_hbm, wov_hbm, wqp_hbm, wkp_hbm, wvp_hbm, wop_hbm)
    loads = [pltpu.make_async_copy(w, weight_ref.at[i], load_sem.at[i]) for i, w in enumerate(weights_hbm)]
    loads.append(pltpu.make_async_copy(cot_hbm, cot_ref, load_sem.at[len(weights_hbm)]))
    for load in loads:
        load.start()

    barrier = pltpu.get_barrier_semaphore()
    peers = [lax.rem(level + k, levels) for k in range(1, levels)]
    around = [lax.rem(place + k, cycle) for k in range(1, cycle)]
    for peer in peers:
        pl.semaphore_signal(barrier, inc=1, device_id={"level": peer}, device_id_type=pl.DeviceIdType.MESH)
    for peer in around:
        pl.semaphore_signal(barrier, inc=1, device_id={"space": peer}, device_id_type=pl.DeviceIdType.MESH)
    pl.semaphore_wait(barrier, levels - 1 + cycle - 1)

    inward, back, halo = [], [], []

    def send_in(c):
        steps = []
        for k, peer in enumerate(peers):
            steps.append(remote(x_ref.at[c, peer], in_ref.at[c, level], in_send.at[c, k], in_recv.at[c, k],
                                {"level": peer}))
            steps[-1].start()
        in_ref[c, level] = x_ref[c, level]
        inward.append(steps)

    for c in range(min(2, chunks)):
        send_in(c)

    lane = lax.broadcasted_iota(jnp.int32, (1, LANES), 1)
    bias_rows = []
    for i in range(levels):
        for j in range(levels):
            row = jnp.zeros((1, LANES), jnp.float32)
            for h in range(lb_ref.shape[2]):
                row = jnp.where(lane == h, lb_ref[i, j, h], row)
            bias_rows.append(row)
    for load in loads[:4]:
        load.wait()

    def vertical_step(c):
        for step in inward[c]:
            step.wait_recv()
        hsend_ref[c] = vertical(in_ref[c], nv_ref[...][None], weight_ref[0], weight_ref[1], weight_ref[2],
                                weight_ref[3], bias_rows, attn_ref.at[pl.ds(0, levels * columns)])
        steps = []
        for k, peer in enumerate(peers):
            steps.append(remote(hsend_ref.at[c, peer], hid_ref.at[c, level], back_send.at[c, k], back_recv.at[c, k],
                                {"level": peer}))
            steps[-1].start()
        hid_ref[c, level] = hsend_ref[c, level]
        back.append(steps)
        if c + 2 < chunks:
            send_in(c + 2)

    toward = lax.rem(place, 2) * 2 - 1
    sources = [lax.rem(place + step * toward + 2 * cycle, cycle) for step in (1, 2, -1, -2)]
    partner = sources[2]
    patches = chunks // SPLIT
    far = len(sources) * patches
    scale = jnp.bfloat16(HD ** (-0.5))

    def halo_step(c):
        for step in back[c]:
            step.wait_recv()
        own_ref[c] = normalized(
            hid_ref[c].reshape(levels * columns, features).astype(jnp.float32), np_ref[...][None]
        )
        steps = []
        for slot, target in ((0, sources[0]), (1, sources[3]), (2, partner)):
            steps.append(remote(own_ref.at[c], far_ref.at[slot * chunks + c], halo_send.at[c, slot],
                                halo_recv.at[c, slot], {"space": target}))
            steps[-1].start()
        halo.append(steps)

    def own_step(patch):
        normed = own_ref[patch * SPLIT : (patch + 1) * SPLIT].reshape(PATCH, features)
        q_ref[pl.ds(patch * PATCH, PATCH), :] = project(normed, weight_ref[4]) * scale
        k_ref[far + patch] = project(normed, weight_ref[5])
        v_ref[far + patch] = project(normed, weight_ref[6])

    def forward(c):
        halo[c][0].wait_recv()
        passed = remote(far_ref.at[c], far_ref.at[3 * chunks + c], halo_send.at[c, 3], halo_recv.at[c, 3],
                        {"space": partner})
        passed.start()
        halo[c].append(passed)

    def distant(slot, patch):
        if slot:
            for c in range(patch * SPLIT, (patch + 1) * SPLIT):
                halo[c][slot].wait_recv()
        start = slot * chunks + patch * SPLIT
        block = far_ref[start : start + SPLIT].reshape(PATCH, features)
        k_ref[slot * patches + patch] = project(block, weight_ref[5])
        v_ref[slot * patches + patch] = project(block, weight_ref[6])

    loaded = False
    for c in range(chunks):
        vertical_step(c)
        if c >= 1:
            halo_step(c - 1)
        if not loaded:
            for load in loads[4:]:
                load.wait()
            loaded = True
    for patch in range(patches - 1):
        own_step(patch)
        distant(2, patch)
    halo_step(chunks - 1)
    for c in range(chunks - SPLIT):
        forward(c)
    own_step(patches - 1)
    for patch in range(patches - 1):
        for slot in (0, 1, 3):
            distant(slot, patch)
    distant(2, patches - 1)
    for c in range(chunks - SPLIT, chunks):
        forward(c)
    for slot in (0, 1, 3):
        distant(slot, patches - 1)

    share = features // cycle
    grain = gsend_ref.shape[1]
    per_pair = LANES // grain
    per_owner = share // grain
    pairs = features // LANES
    tables = [[choices(nb_ref, count_ref, patch, source, patches) for source in sources] for patch in range(patches)]

    def share_of(index):
        owner = index // per_owner
        part = lax.rem(index, per_owner)
        gap = lax.rem(place - owner + cycle, cycle)
        slot = jnp.maximum(gap - 1, 0) * per_owner + part
        return owner, remote(gsend_ref.at[index], grecv_ref.at[slot], share_send.at[index], share_recv.at[slot],
                             {"space": owner})

    def pair(turn, carry):
        step = lax.rem(place * pairs // cycle + 1 + turn, pairs)
        attend(step, q_ref, k_ref, v_ref, attn_ref, pb_ref, tables, far)
        lanes = pl.ds(pl.multiple_of(step * LANES, LANES), LANES)
        total = lax.dot_general(
            attn_ref[:, lanes], cot_ref[...], (((0,), (0,)), ((), ())), preferred_element_type=jnp.float32
        ).astype(jnp.bfloat16)
        for part in range(per_pair):
            gsend_ref[step * per_pair + part] = total[part * grain : (part + 1) * grain]
        for part in range(per_pair):
            owner, copy = share_of(step * per_pair + part)

            @pl.when(owner != place)
            def _():
                copy.start()

        return carry

    lax.fori_loop(0, pairs, pair, 0)
    out_ref[...] = (
        hid_ref[...].reshape(patches * PATCH, features).astype(jnp.float32)
        + jnp.dot(attn_ref[...], weight_ref[7], preferred_element_type=jnp.float32)
    ).astype(jnp.bfloat16)
    sums = []
    for part in range(per_owner):
        sums.append(gsend_ref[place * per_owner + part].astype(jnp.float32))
        for k in range(cycle - 1):
            slot = k * per_owner + part
            remote(gsend_ref.at[0], grecv_ref.at[slot], share_send.at[0], share_recv.at[slot],
                   {"space": partner}).wait_recv()
            sums[-1] = sums[-1] + grecv_ref[slot].astype(jnp.float32)
    gathered = jnp.concatenate(sums, axis=0)
    piece = share // levels
    for i in range(levels):
        lsend_ref[i] = gathered[i * piece : (i + 1) * piece].astype(jnp.bfloat16)
    parts = []
    for k, peer in enumerate(peers):
        parts.append(remote(lsend_ref.at[peer], lrecv_ref.at[k], part_send.at[k], part_recv.at[k], {"level": peer}))
        parts[-1].start()
    gathered = lsend_ref[level].astype(jnp.float32)
    for k, step in enumerate(parts):
        step.wait_recv()
        gathered = gathered + lrecv_ref[k].astype(jnp.float32)
    final_ref[level] = gathered.astype(jnp.bfloat16)
    fulls = []
    for k, peer in enumerate(peers):
        fulls.append(remote(final_ref.at[level], final_ref.at[level], full_send.at[k], full_recv.at[k],
                            {"level": peer}))
        fulls[-1].start()
    for step in fulls:
        step.wait_recv()
    for i in range(levels):
        grad_ref[i * piece : (i + 1) * piece, :] = final_ref[i].astype(jnp.float32)
    for steps in inward + back + halo + [parts, fulls]:
        for step in steps:
            step.wait_send()

    def drained(index, carry):
        owner, copy = share_of(index)

        @pl.when(owner != place)
        def _():
            copy.wait_send()

        return carry

    lax.fori_loop(0, pairs * per_pair, drained, 0)


def body(fields, norm_vert, query_vert, keys_vert, values_vert, out_vert, level_bias, norm_patch, query_patch,
         keys_patch, values_patch, out_patch, patch_bias, neighbours, counts, cotangent):
    _, tokens, features = fields.shape
    levels = lax.axis_size("level")
    cycle = lax.axis_size("space")
    patches = tokens // PATCH
    chunks = patches * SPLIT
    columns = PATCH // SPLIT // levels
    grain = math.gcd(features // cycle, LANES)
    share = features // cycle
    x = fields.reshape(chunks, levels, columns, features)
    vmem = pl.BlockSpec(memory_space=pltpu.VMEM)
    smem = pl.BlockSpec(memory_space=pltpu.SMEM)
    hbm = pl.BlockSpec(memory_space=pl.ANY)
    narrow = lambda *shape: pltpu.VMEM(shape, jnp.bfloat16)
    dma = lambda *shape: pltpu.SemaphoreType.DMA(shape)
    blocks = 5 * patches
    out, grad = pl.pallas_call(
        functools.partial(whole_kernel, cycle, levels),
        out_shape=(
            jax.ShapeDtypeStruct((tokens, features), jnp.bfloat16),
            jax.ShapeDtypeStruct((share, features), jnp.float32),
        ),
        in_specs=[vmem] * 3 + [hbm] * 9 + [smem] * 4,
        out_specs=(vmem, vmem),
        scratch_shapes=[
            narrow(8, features, features),
            narrow(tokens, features),
            narrow(chunks, levels, columns, features),
            narrow(chunks, levels, columns, features),
            narrow(chunks, levels, columns, features),
            narrow(tokens, features),
            narrow(chunks, PATCH // SPLIT, features),
            narrow(4 * chunks, PATCH // SPLIT, features),
            narrow(tokens, features),
            narrow(blocks, PATCH, features),
            narrow(blocks, PATCH, features),
            narrow(features // grain, grain, features),
            narrow((cycle - 1) * share // grain, grain, features),
            narrow(levels, share // levels, features),
            narrow(levels - 1, share // levels, features),
            narrow(levels, share // levels, features),
            dma(9),
            dma(chunks, levels - 1),
            dma(chunks, levels - 1),
            dma(chunks, levels - 1),
            dma(chunks, levels - 1),
            dma(chunks, 4),
            dma(chunks, 4),
            dma(features // grain),
            dma((cycle - 1) * share // grain),
            dma(levels - 1),
            dma(levels - 1),
            dma(levels - 1),
            dma(levels - 1),
        ],
        compiler_params=pltpu.CompilerParams(
            collective_id=0, has_side_effects=True, vmem_limit_bytes=VMEM_LIMIT
        ),
        name="whole_block",
    )(x, norm_vert, norm_patch, query_vert, keys_vert, values_vert, out_vert, query_patch, keys_patch,
      values_patch, out_patch, cotangent[0], jnp.transpose(level_bias, (1, 2, 0)), patch_bias.T, neighbours, counts)
    return (out[None], grad)


def solution(mesh):
    split = P("level", "space", None)
    return jax.shard_map(
        body,
        mesh=mesh,
        in_specs=(split,) + (P(),) * 12 + (P("space", None), P("space"), split),
        out_specs=(split, P("space", None)),
        check_vma=False,
    )
```

```python
import functools
import math

import jax
import jax.numpy as jnp
from jax import lax
from jax.experimental import pallas as pl
from jax.experimental.pallas import tpu as pltpu
from jax.sharding import PartitionSpec as P

HD = 64
PATCH = 256
LANES = 128
SPLIT = 2
VMEM_LIMIT = 58 * 1024 * 1024

epsilon = 1e-06


def normalized(widened, scaling):
    mean_square = jnp.mean(widened * widened, axis=-1, keepdims=True)
    return (widened * lax.rsqrt(mean_square + epsilon) * scaling).astype(jnp.bfloat16)


def project(inputs, weight):
    return jnp.dot(inputs, weight, preferred_element_type=jnp.float32).astype(jnp.bfloat16)


def vertical(x, gain, wq, wk, wv, wo, bias_rows, attn_ref):
    levels, columns, features = x.shape
    tokens = levels * columns
    x = x.reshape(tokens, features).astype(jnp.float32)
    normed = normalized(x, gain)
    queries = project(normed, wq).astype(jnp.float32)
    keys = project(normed, wk).astype(jnp.float32)
    values = project(normed, wv).astype(jnp.float32)
    head_of = lax.broadcasted_iota(jnp.int32, (features, LANES), 0) // HD
    gather_heads = (head_of == lax.broadcasted_iota(jnp.int32, (features, LANES), 1)).astype(jnp.bfloat16)
    head_to = lax.broadcasted_iota(jnp.int32, (LANES, features), 1) // HD
    spread_heads = (head_to == lax.broadcasted_iota(jnp.int32, (LANES, features), 0)).astype(jnp.bfloat16)
    for i in range(levels):
        query = queries[i * columns : (i + 1) * columns]
        products = jnp.concatenate(
            [(query * keys[j * columns : (j + 1) * columns]).astype(jnp.bfloat16) for j in range(levels)], axis=0
        )
        summed = jnp.dot(products, gather_heads, preferred_element_type=jnp.float32) * HD ** (-0.5)
        scores = [
            summed[j * columns : (j + 1) * columns] + bias_rows[i * levels + j]
            for j in range(levels)
        ]
        top = functools.reduce(jnp.maximum, scores)
        raised = [jnp.exp(score - top) for score in scores]
        inverse = 1.0 / functools.reduce(jnp.add, raised)
        weights = jnp.concatenate([(each * inverse).astype(jnp.bfloat16) for each in raised], axis=0)
        spread = jnp.dot(weights, spread_heads, preferred_element_type=jnp.float32)
        mixed = functools.reduce(
            jnp.add,
            [
                spread[j * columns : (j + 1) * columns] * values[j * columns : (j + 1) * columns]
                for j in range(levels)
            ],
        )
        attn_ref[i * columns : (i + 1) * columns, :] = mixed.astype(jnp.bfloat16)
    hidden = x + jnp.dot(attn_ref[...], wo, preferred_element_type=jnp.float32)
    return hidden.astype(jnp.bfloat16).reshape(levels, columns, features)


def choices(nb_ref, count_ref, patch, source, per_device):
    live = jnp.int32(0)
    within = jnp.int32(0)
    for m in range(nb_ref.shape[1]):
        listed = jnp.maximum(nb_ref[patch, m], 0)
        hit = jnp.logical_and(m < count_ref[patch], lax.div(listed, per_device) == source)
        live = jnp.where(hit, 1, live)
        within = jnp.where(hit, lax.rem(listed, per_device), within)
    return live, within


def attend(step, q_ref, k_ref, v_ref, attn_ref, pb_ref, tables, far, slots, early, top_ref, total_ref, mixed_ref):
    low = lax.broadcasted_iota(jnp.int32, (1, LANES), 1) < HD
    lanes = pl.ds(pl.multiple_of(step * LANES, LANES), LANES)
    for patch, picked in enumerate(tables):
        rows = pl.ds(patch * PATCH, PATCH)
        blocks = [slot * len(tables) + picked[slot][1] for slot in slots]
        if early:
            blocks = [far + patch] + blocks
        query = q_ref[rows, lanes]
        results = []
        for parity in range(2):
            head = step * 2 + parity
            mine = low if parity == 0 else jnp.logical_not(low)
            masked = jnp.where(mine, query, jnp.zeros_like(query))
            scores = [
                lax.dot_general(
                    masked, k_ref[block, :, lanes], (((1,), (1,)), ((), ())), preferred_element_type=jnp.float32
                )
                for block in blocks
            ]
            adds = [jnp.where(picked[slot][0] > 0, pb_ref[1, head], jnp.float32(-1e30)) for slot in slots]
            if early:
                adds = [pb_ref[0, head]] + adds
            top = functools.reduce(
                jnp.maximum, [jnp.max(s, axis=-1, keepdims=True) + a for s, a in zip(scores, adds)]
            )
            if not early:
                before = top_ref[rows, lanes][:, parity * HD : parity * HD + 1]
                top = jnp.maximum(top, before)
            raised = [jnp.exp(s + (a - top)) for s, a in zip(scores, adds)]
            total = functools.reduce(jnp.add, [jnp.sum(r, axis=-1, keepdims=True) for r in raised])
            mixed = functools.reduce(
                jnp.add,
                [
                    jnp.dot(r.astype(jnp.bfloat16), v_ref[block, :, lanes], preferred_element_type=jnp.float32)
                    for r, block in zip(raised, blocks)
                ],
            )
            if early:
                results.append((top, total, mixed))
            else:
                fade = jnp.exp(before - top)
                total = total + total_ref[rows, lanes][:, parity * HD : parity * HD + 1] * fade
                results.append((mixed + mixed_ref[rows, lanes] * fade) / total)
        if early:
            for ref, even, odd in zip((top_ref, total_ref, mixed_ref), *results):
                ref[rows, lanes] = jnp.where(low, even, odd)
        else:
            attn_ref[rows, lanes] = jnp.where(low, results[0], results[1]).astype(jnp.bfloat16)


def remote(src, dst, send, recv, device):
    return pltpu.make_async_remote_copy(
        src_ref=src, dst_ref=dst, send_sem=send, recv_sem=recv, device_id=device,
        device_id_type=pl.DeviceIdType.MESH,
    )


def whole_kernel(cycle, levels, x_ref, nv_ref, np_ref, wqv_hbm, wkv_hbm, wvv_hbm, wov_hbm, wqp_hbm, wkp_hbm, wvp_hbm,
                 wop_hbm, cot_hbm, lb_ref, pb_ref, nb_ref, count_ref, out_ref, grad_ref, weight_ref, cot_ref, in_ref,
                 hsend_ref, hid_ref, attn_ref, own_ref, far_ref, q_ref, k_ref, v_ref, gsend_ref, grecv_ref, lsend_ref,
                 lrecv_ref, final_ref, top_ref, total_ref, mixed_ref, load_sem, in_send, in_recv, back_send, back_recv, halo_send, halo_recv,
                 share_send, share_recv, part_send, part_recv, full_send, full_recv):
    chunks, _, columns, features = x_ref.shape
    place = lax.axis_index("space")
    level = lax.axis_index("level")
    weights_hbm = (wqv_hbm, wkv_hbm, wvv_hbm, wov_hbm, wqp_hbm, wkp_hbm, wvp_hbm, wop_hbm)
    loads = [pltpu.make_async_copy(w, weight_ref.at[i], load_sem.at[i]) for i, w in enumerate(weights_hbm)]
    loads.append(pltpu.make_async_copy(cot_hbm, cot_ref, load_sem.at[len(weights_hbm)]))
    for load in loads:
        load.start()

    barrier = pltpu.get_barrier_semaphore()
    peers = [lax.rem(level + k, levels) for k in range(1, levels)]
    around = [lax.rem(place + k, cycle) for k in range(1, cycle)]
    for peer in peers:
        pl.semaphore_signal(barrier, inc=1, device_id={"level": peer}, device_id_type=pl.DeviceIdType.MESH)
    for peer in around:
        pl.semaphore_signal(barrier, inc=1, device_id={"space": peer}, device_id_type=pl.DeviceIdType.MESH)
    pl.semaphore_wait(barrier, levels - 1 + cycle - 1)

    inward, back, halo = [], [], []

    def send_in(c):
        steps = []
        for k, peer in enumerate(peers):
            steps.append(remote(x_ref.at[c, peer], in_ref.at[c, level], in_send.at[c, k], in_recv.at[c, k],
                                {"level": peer}))
            steps[-1].start()
        in_ref[c, level] = x_ref[c, level]
        inward.append(steps)

    for c in range(min(2, chunks)):
        send_in(c)

    lane = lax.broadcasted_iota(jnp.int32, (1, LANES), 1)
    bias_rows = []
    for i in range(levels):
        for j in range(levels):
            row = jnp.zeros((1, LANES), jnp.float32)
            for h in range(lb_ref.shape[2]):
                row = jnp.where(lane == h, lb_ref[i, j, h], row)
            bias_rows.append(row)
    for load in loads[:4]:
        load.wait()

    def vertical_step(c):
        for step in inward[c]:
            step.wait_recv()
        hsend_ref[c] = vertical(in_ref[c], nv_ref[...][None], weight_ref[0], weight_ref[1], weight_ref[2],
                                weight_ref[3], bias_rows, attn_ref.at[pl.ds(0, levels * columns)])
        steps = []
        for k, peer in enumerate(peers):
            steps.append(remote(hsend_ref.at[c, peer], hid_ref.at[c, level], back_send.at[c, k], back_recv.at[c, k],
                                {"level": peer}))
            steps[-1].start()
        hid_ref[c, level] = hsend_ref[c, level]
        back.append(steps)
        if c + 2 < chunks:
            send_in(c + 2)

    toward = lax.rem(place, 2) * 2 - 1
    sources = [lax.rem(place + step * toward + 2 * cycle, cycle) for step in (1, 2, -1, -2)]
    partner = sources[2]
    patches = chunks // SPLIT
    far = len(sources) * patches
    scale = jnp.bfloat16(HD ** (-0.5))

    def halo_step(c):
        for step in back[c]:
            step.wait_recv()
        own_ref[c] = normalized(
            hid_ref[c].reshape(levels * columns, features).astype(jnp.float32), np_ref[...][None]
        )
        steps = []
        for slot, target in ((0, sources[0]), (1, sources[3]), (2, partner)):
            steps.append(remote(own_ref.at[c], far_ref.at[slot * chunks + c], halo_send.at[c, slot],
                                halo_recv.at[c, slot], {"space": target}))
            steps[-1].start()
        halo.append(steps)

    def own_step(patch):
        normed = own_ref[patch * SPLIT : (patch + 1) * SPLIT].reshape(PATCH, features)
        q_ref[pl.ds(patch * PATCH, PATCH), :] = project(normed, weight_ref[4]) * scale
        k_ref[far + patch] = project(normed, weight_ref[5])
        v_ref[far + patch] = project(normed, weight_ref[6])

    def forward(c):
        halo[c][0].wait_recv()
        passed = remote(far_ref.at[c], far_ref.at[3 * chunks + c], halo_send.at[c, 3], halo_recv.at[c, 3],
                        {"space": partner})
        passed.start()
        halo[c].append(passed)

    def distant(slot, patch):
        if slot:
            for c in range(patch * SPLIT, (patch + 1) * SPLIT):
                halo[c][slot].wait_recv()
        start = slot * chunks + patch * SPLIT
        block = far_ref[start : start + SPLIT].reshape(PATCH, features)
        k_ref[slot * patches + patch] = project(block, weight_ref[5])
        v_ref[slot * patches + patch] = project(block, weight_ref[6])

    loaded = False
    for c in range(chunks):
        vertical_step(c)
        if c >= 1:
            halo_step(c - 1)
        if not loaded:
            for load in loads[4:]:
                load.wait()
            loaded = True
    for patch in range(patches - 1):
        own_step(patch)
        distant(2, patch)
    halo_step(chunks - 1)
    for c in range(chunks - SPLIT):
        forward(c)
    own_step(patches - 1)
    distant(2, patches - 1)
    for patch in range(patches - 1):
        for slot in (0, 1, 3):
            distant(slot, patch)
    pairs = features // LANES
    tables = [[choices(nb_ref, count_ref, patch, source, patches) for source in sources] for patch in range(patches)]
    states = (top_ref, total_ref, mixed_ref)

    def early_pair(step, carry):
        attend(step, q_ref, k_ref, v_ref, attn_ref, pb_ref, tables, far, (2,), True, *states)
        return carry

    for c in range(chunks - SPLIT, chunks - 1):
        forward(c)
    lax.fori_loop(0, pairs, early_pair, 0)
    forward(chunks - 1)
    for slot in (0, 1, 3):
        distant(slot, patches - 1)

    share = features // cycle
    grain = gsend_ref.shape[1]
    per_pair = LANES // grain
    per_owner = share // grain

    def share_of(index):
        owner = index // per_owner
        part = lax.rem(index, per_owner)
        gap = lax.rem(place - owner + cycle, cycle)
        slot = jnp.maximum(gap - 1, 0) * per_owner + part
        return owner, remote(gsend_ref.at[index], grecv_ref.at[slot], share_send.at[index], share_recv.at[slot],
                             {"space": owner})

    def pair(turn, carry):
        step = lax.rem(place * pairs // cycle + 1 + turn, pairs)
        attend(step, q_ref, k_ref, v_ref, attn_ref, pb_ref, tables, far, (0, 1, 3), False, *states)
        lanes = pl.ds(pl.multiple_of(step * LANES, LANES), LANES)
        total = lax.dot_general(
            attn_ref[:, lanes], cot_ref[...], (((0,), (0,)), ((), ())), preferred_element_type=jnp.float32
        ).astype(jnp.bfloat16)
        for part in range(per_pair):
            gsend_ref[step * per_pair + part] = total[part * grain : (part + 1) * grain]
        for part in range(per_pair):
            owner, copy = share_of(step * per_pair + part)

            @pl.when(owner != place)
            def _():
                copy.start()

        return carry

    lax.fori_loop(0, pairs, pair, 0)
    out_ref[...] = (
        hid_ref[...].reshape(patches * PATCH, features).astype(jnp.float32)
        + jnp.dot(attn_ref[...], weight_ref[7], preferred_element_type=jnp.float32)
    ).astype(jnp.bfloat16)
    sums = []
    for part in range(per_owner):
        sums.append(gsend_ref[place * per_owner + part].astype(jnp.float32))
        for k in range(cycle - 1):
            slot = k * per_owner + part
            remote(gsend_ref.at[0], grecv_ref.at[slot], share_send.at[0], share_recv.at[slot],
                   {"space": partner}).wait_recv()
            sums[-1] = sums[-1] + grecv_ref[slot].astype(jnp.float32)
    gathered = jnp.concatenate(sums, axis=0)
    piece = share // levels
    for i in range(levels):
        lsend_ref[i] = gathered[i * piece : (i + 1) * piece].astype(jnp.bfloat16)
    parts = []
    for k, peer in enumerate(peers):
        parts.append(remote(lsend_ref.at[peer], lrecv_ref.at[k], part_send.at[k], part_recv.at[k], {"level": peer}))
        parts[-1].start()
    gathered = lsend_ref[level].astype(jnp.float32)
    for k, step in enumerate(parts):
        step.wait_recv()
        gathered = gathered + lrecv_ref[k].astype(jnp.float32)
    final_ref[level] = gathered.astype(jnp.bfloat16)
    fulls = []
    for k, peer in enumerate(peers):
        fulls.append(remote(final_ref.at[level], final_ref.at[level], full_send.at[k], full_recv.at[k],
                            {"level": peer}))
        fulls[-1].start()
    for step in fulls:
        step.wait_recv()
    for i in range(levels):
        grad_ref[i * piece : (i + 1) * piece, :] = final_ref[i].astype(jnp.float32)
    for steps in inward + back + halo + [parts, fulls]:
        for step in steps:
            step.wait_send()

    def drained(index, carry):
        owner, copy = share_of(index)

        @pl.when(owner != place)
        def _():
            copy.wait_send()

        return carry

    lax.fori_loop(0, pairs * per_pair, drained, 0)


def body(fields, norm_vert, query_vert, keys_vert, values_vert, out_vert, level_bias, norm_patch, query_patch,
         keys_patch, values_patch, out_patch, patch_bias, neighbours, counts, cotangent):
    _, tokens, features = fields.shape
    levels = lax.axis_size("level")
    cycle = lax.axis_size("space")
    patches = tokens // PATCH
    chunks = patches * SPLIT
    columns = PATCH // SPLIT // levels
    grain = math.gcd(features // cycle, LANES)
    share = features // cycle
    x = fields.reshape(chunks, levels, columns, features)
    vmem = pl.BlockSpec(memory_space=pltpu.VMEM)
    smem = pl.BlockSpec(memory_space=pltpu.SMEM)
    hbm = pl.BlockSpec(memory_space=pl.ANY)
    narrow = lambda *shape: pltpu.VMEM(shape, jnp.bfloat16)
    dma = lambda *shape: pltpu.SemaphoreType.DMA(shape)
    blocks = 5 * patches
    out, grad = pl.pallas_call(
        functools.partial(whole_kernel, cycle, levels),
        out_shape=(
            jax.ShapeDtypeStruct((tokens, features), jnp.bfloat16),
            jax.ShapeDtypeStruct((share, features), jnp.float32),
        ),
        in_specs=[vmem] * 3 + [hbm] * 9 + [smem] * 4,
        out_specs=(vmem, vmem),
        scratch_shapes=[
            narrow(8, features, features),
            narrow(tokens, features),
            narrow(chunks, levels, columns, features),
            narrow(chunks, levels, columns, features),
            narrow(chunks, levels, columns, features),
            narrow(tokens, features),
            narrow(chunks, PATCH // SPLIT, features),
            narrow(4 * chunks, PATCH // SPLIT, features),
            narrow(tokens, features),
            narrow(blocks, PATCH, features),
            narrow(blocks, PATCH, features),
            narrow(features // grain, grain, features),
            narrow((cycle - 1) * share // grain, grain, features),
            narrow(levels, share // levels, features),
            narrow(levels - 1, share // levels, features),
            narrow(levels, share // levels, features),
            pltpu.VMEM((tokens, features), jnp.float32),
            pltpu.VMEM((tokens, features), jnp.float32),
            pltpu.VMEM((tokens, features), jnp.float32),
            dma(9),
            dma(chunks, levels - 1),
            dma(chunks, levels - 1),
            dma(chunks, levels - 1),
            dma(chunks, levels - 1),
            dma(chunks, 4),
            dma(chunks, 4),
            dma(features // grain),
            dma((cycle - 1) * share // grain),
            dma(levels - 1),
            dma(levels - 1),
            dma(levels - 1),
            dma(levels - 1),
        ],
        compiler_params=pltpu.CompilerParams(
            collective_id=0, has_side_effects=True, vmem_limit_bytes=VMEM_LIMIT
        ),
        name="whole_block",
    )(x, norm_vert, norm_patch, query_vert, keys_vert, values_vert, out_vert, query_patch, keys_patch,
      values_patch, out_patch, cotangent[0], jnp.transpose(level_bias, (1, 2, 0)), patch_bias.T, neighbours, counts)
    return (out[None], grad)


def solution(mesh):
    split = P("level", "space", None)
    return jax.shard_map(
        body,
        mesh=mesh,
        in_specs=(split,) + (P(),) * 12 + (P("space", None), P("space"), split),
        out_specs=(split, P("space", None)),
        check_vma=False,
    )
```

```python
import functools
import math

import jax
import jax.numpy as jnp
from jax import lax
from jax.experimental import pallas as pl
from jax.experimental.pallas import tpu as pltpu
from jax.sharding import PartitionSpec as P

HD = 64
PATCH = 256
LANES = 128
SPLIT = 2
VMEM_LIMIT = 58 * 1024 * 1024

epsilon = 1e-06


def normalized(widened, scaling):
    mean_square = jnp.mean(widened * widened, axis=-1, keepdims=True)
    return (widened * lax.rsqrt(mean_square + epsilon) * scaling).astype(jnp.bfloat16)


def project(inputs, weight):
    return jnp.dot(inputs, weight, preferred_element_type=jnp.float32).astype(jnp.bfloat16)


def vertical(x, gain, wq, wk, wv, wo, bias_rows, attn_ref):
    levels, columns, features = x.shape
    tokens = levels * columns
    x = x.reshape(tokens, features).astype(jnp.float32)
    normed = normalized(x, gain)
    queries = project(normed, wq).astype(jnp.float32)
    keys = project(normed, wk).astype(jnp.float32)
    values = project(normed, wv).astype(jnp.float32)
    head_of = lax.broadcasted_iota(jnp.int32, (features, LANES), 0) // HD
    gather_heads = (head_of == lax.broadcasted_iota(jnp.int32, (features, LANES), 1)).astype(jnp.bfloat16)
    head_to = lax.broadcasted_iota(jnp.int32, (LANES, features), 1) // HD
    spread_heads = (head_to == lax.broadcasted_iota(jnp.int32, (LANES, features), 0)).astype(jnp.bfloat16)
    for i in range(levels):
        query = queries[i * columns : (i + 1) * columns]
        products = jnp.concatenate(
            [(query * keys[j * columns : (j + 1) * columns]).astype(jnp.bfloat16) for j in range(levels)], axis=0
        )
        summed = jnp.dot(products, gather_heads, preferred_element_type=jnp.float32) * HD ** (-0.5)
        scores = [
            summed[j * columns : (j + 1) * columns] + bias_rows[i * levels + j]
            for j in range(levels)
        ]
        top = functools.reduce(jnp.maximum, scores)
        raised = [jnp.exp(score - top) for score in scores]
        inverse = 1.0 / functools.reduce(jnp.add, raised)
        weights = jnp.concatenate([(each * inverse).astype(jnp.bfloat16) for each in raised], axis=0)
        spread = jnp.dot(weights, spread_heads, preferred_element_type=jnp.float32)
        mixed = functools.reduce(
            jnp.add,
            [
                spread[j * columns : (j + 1) * columns] * values[j * columns : (j + 1) * columns]
                for j in range(levels)
            ],
        )
        attn_ref[i * columns : (i + 1) * columns, :] = mixed.astype(jnp.bfloat16)
    hidden = x + jnp.dot(attn_ref[...], wo, preferred_element_type=jnp.float32)
    return hidden.astype(jnp.bfloat16).reshape(levels, columns, features)


def choices(nb_ref, count_ref, patch, source, per_device):
    live = jnp.int32(0)
    within = jnp.int32(0)
    for m in range(nb_ref.shape[1]):
        listed = jnp.maximum(nb_ref[patch, m], 0)
        hit = jnp.logical_and(m < count_ref[patch], lax.div(listed, per_device) == source)
        live = jnp.where(hit, 1, live)
        within = jnp.where(hit, lax.rem(listed, per_device), within)
    return live, within


def attend(step, q_ref, k_ref, v_ref, attn_ref, pb_ref, tables, far, slots, early, top_ref, total_ref, mixed_ref):
    low = lax.broadcasted_iota(jnp.int32, (1, LANES), 1) < HD
    lanes = pl.ds(pl.multiple_of(step * LANES, LANES), LANES)
    for patch, picked in enumerate(tables):
        rows = pl.ds(patch * PATCH, PATCH)
        blocks = [slot * len(tables) + picked[slot][1] for slot in slots]
        if early:
            blocks = [far + patch] + blocks
        query = q_ref[rows, lanes]
        results = []
        for parity in range(2):
            head = step * 2 + parity
            mine = low if parity == 0 else jnp.logical_not(low)
            masked = jnp.where(mine, query, jnp.zeros_like(query))
            scores = [
                lax.dot_general(
                    masked, k_ref[block, :, lanes], (((1,), (1,)), ((), ())), preferred_element_type=jnp.float32
                )
                for block in blocks
            ]
            adds = [jnp.where(picked[slot][0] > 0, pb_ref[1, head], jnp.float32(-1e30)) for slot in slots]
            if early:
                adds = [pb_ref[0, head]] + adds
            top = functools.reduce(
                jnp.maximum, [jnp.max(s, axis=-1, keepdims=True) + a for s, a in zip(scores, adds)]
            )
            if not early:
                before = top_ref[rows, lanes][:, parity * HD : parity * HD + 1]
                top = jnp.maximum(top, before)
            raised = [jnp.exp(s + (a - top)) for s, a in zip(scores, adds)]
            total = functools.reduce(jnp.add, [jnp.sum(r, axis=-1, keepdims=True) for r in raised])
            mixed = functools.reduce(
                jnp.add,
                [
                    jnp.dot(r.astype(jnp.bfloat16), v_ref[block, :, lanes], preferred_element_type=jnp.float32)
                    for r, block in zip(raised, blocks)
                ],
            )
            if early:
                results.append((top, total, mixed))
            else:
                fade = jnp.exp(before - top)
                total = total + total_ref[rows, lanes][:, parity * HD : parity * HD + 1] * fade
                results.append((mixed + mixed_ref[rows, lanes] * fade) / total)
        if early:
            for ref, even, odd in zip((top_ref, total_ref, mixed_ref), *results):
                ref[rows, lanes] = jnp.where(low, even, odd)
        else:
            attn_ref[rows, lanes] = jnp.where(low, results[0], results[1]).astype(jnp.bfloat16)


def remote(src, dst, send, recv, device):
    return pltpu.make_async_remote_copy(
        src_ref=src, dst_ref=dst, send_sem=send, recv_sem=recv, device_id=device,
        device_id_type=pl.DeviceIdType.MESH,
    )


def whole_kernel(cycle, levels, x_ref, nv_ref, np_ref, wqv_hbm, wkv_hbm, wvv_hbm, wov_hbm, wqp_hbm, wkp_hbm, wvp_hbm,
                 wop_hbm, cot_hbm, lb_ref, pb_ref, nb_ref, count_ref, out_ref, grad_ref, weight_ref, cot_ref, in_ref,
                 hsend_ref, hid_ref, attn_ref, own_ref, far_ref, q_ref, k_ref, v_ref, gsend_ref, grecv_ref, lsend_ref,
                 lrecv_ref, final_ref, top_ref, total_ref, mixed_ref, load_sem, in_send, in_recv, back_send, back_recv, halo_send, halo_recv,
                 share_send, share_recv, part_send, part_recv, full_send, full_recv):
    chunks, _, columns, features = x_ref.shape
    place = lax.axis_index("space")
    level = lax.axis_index("level")
    weights_hbm = (wqv_hbm, wkv_hbm, wvv_hbm, wov_hbm, wqp_hbm, wkp_hbm, wvp_hbm, wop_hbm)
    loads = [pltpu.make_async_copy(w, weight_ref.at[i], load_sem.at[i]) for i, w in enumerate(weights_hbm)]
    loads.append(pltpu.make_async_copy(cot_hbm, cot_ref, load_sem.at[len(weights_hbm)]))
    for load in loads:
        load.start()

    barrier = pltpu.get_barrier_semaphore()
    peers = [lax.rem(level + k, levels) for k in range(1, levels)]
    around = [lax.rem(place + k, cycle) for k in range(1, cycle)]
    for peer in peers:
        pl.semaphore_signal(barrier, inc=1, device_id={"level": peer}, device_id_type=pl.DeviceIdType.MESH)
    for peer in around:
        pl.semaphore_signal(barrier, inc=1, device_id={"space": peer}, device_id_type=pl.DeviceIdType.MESH)
    pl.semaphore_wait(barrier, levels - 1 + cycle - 1)

    inward, back, halo = [], [], []

    def send_in(c):
        steps = []
        for k, peer in enumerate(peers):
            steps.append(remote(x_ref.at[c, peer], in_ref.at[c, level], in_send.at[c, k], in_recv.at[c, k],
                                {"level": peer}))
            steps[-1].start()
        in_ref[c, level] = x_ref[c, level]
        inward.append(steps)

    for c in range(min(2, chunks)):
        send_in(c)

    lane = lax.broadcasted_iota(jnp.int32, (1, LANES), 1)
    bias_rows = []
    for i in range(levels):
        for j in range(levels):
            row = jnp.zeros((1, LANES), jnp.float32)
            for h in range(lb_ref.shape[2]):
                row = jnp.where(lane == h, lb_ref[i, j, h], row)
            bias_rows.append(row)
    for load in loads[:4]:
        load.wait()

    def vertical_step(c):
        for step in inward[c]:
            step.wait_recv()
        hsend_ref[c] = vertical(in_ref[c], nv_ref[...][None], weight_ref[0], weight_ref[1], weight_ref[2],
                                weight_ref[3], bias_rows, attn_ref.at[pl.ds(0, levels * columns)])
        steps = []
        for k, peer in enumerate(peers):
            steps.append(remote(hsend_ref.at[c, peer], hid_ref.at[c, level], back_send.at[c, k], back_recv.at[c, k],
                                {"level": peer}))
            steps[-1].start()
        hid_ref[c, level] = hsend_ref[c, level]
        back.append(steps)
        if c + 2 < chunks:
            send_in(c + 2)

    toward = lax.rem(place, 2) * 2 - 1
    sources = [lax.rem(place + step * toward + 2 * cycle, cycle) for step in (1, 2, -1, -2)]
    partner = sources[2]
    patches = chunks // SPLIT
    far = len(sources) * patches
    scale = jnp.bfloat16(HD ** (-0.5))

    def halo_step(c):
        for step in back[c]:
            step.wait_recv()
        own_ref[c] = normalized(
            hid_ref[c].reshape(levels * columns, features).astype(jnp.float32), np_ref[...][None]
        )
        steps = []
        for slot, target in ((0, sources[0]), (1, sources[3]), (2, partner)):
            steps.append(remote(own_ref.at[c], far_ref.at[slot * chunks + c], halo_send.at[c, slot],
                                halo_recv.at[c, slot], {"space": target}))
            steps[-1].start()
        halo.append(steps)

    def own_step(patch):
        normed = own_ref[patch * SPLIT : (patch + 1) * SPLIT].reshape(PATCH, features)
        q_ref[pl.ds(patch * PATCH, PATCH), :] = project(normed, weight_ref[4]) * scale
        k_ref[far + patch] = project(normed, weight_ref[5])
        v_ref[far + patch] = project(normed, weight_ref[6])

    def forward(c):
        halo[c][0].wait_recv()
        passed = remote(far_ref.at[c], far_ref.at[3 * chunks + c], halo_send.at[c, 3], halo_recv.at[c, 3],
                        {"space": partner})
        passed.start()
        halo[c].append(passed)

    def distant(slot, patch):
        if slot:
            for c in range(patch * SPLIT, (patch + 1) * SPLIT):
                halo[c][slot].wait_recv()
        start = slot * chunks + patch * SPLIT
        block = far_ref[start : start + SPLIT].reshape(PATCH, features)
        k_ref[slot * patches + patch] = project(block, weight_ref[5])
        v_ref[slot * patches + patch] = project(block, weight_ref[6])

    loaded = False
    for c in range(chunks):
        vertical_step(c)
        if c >= 1:
            halo_step(c - 1)
        if not loaded:
            for load in loads[4:]:
                load.wait()
            loaded = True
    for patch in range(patches - 1):
        own_step(patch)
        distant(2, patch)
    halo_step(chunks - 1)
    for c in range(chunks - SPLIT):
        forward(c)
    own_step(patches - 1)
    distant(2, patches - 1)
    for patch in range(patches - 1):
        for slot in (0, 1, 3):
            distant(slot, patch)
    pairs = features // LANES
    tables = [[choices(nb_ref, count_ref, patch, source, patches) for source in sources] for patch in range(patches)]
    states = (top_ref, total_ref, mixed_ref)

    def early_pair(step, carry):
        attend(step, q_ref, k_ref, v_ref, attn_ref, pb_ref, tables, far, (2,), True, *states)
        return carry

    for c in range(chunks - SPLIT, chunks - 1):
        forward(c)
    lax.fori_loop(0, pairs, early_pair, 0)
    forward(chunks - 1)
    for slot in (0, 1, 3):
        distant(slot, patches - 1)

    share = features // cycle
    grain = gsend_ref.shape[1]
    per_pair = LANES // grain
    per_owner = share // grain

    def share_of(index):
        owner = index // per_owner
        part = lax.rem(index, per_owner)
        gap = lax.rem(place - owner + cycle, cycle)
        slot = jnp.maximum(gap - 1, 0) * per_owner + part
        return owner, remote(gsend_ref.at[index], grecv_ref.at[slot], share_send.at[index], share_recv.at[slot],
                             {"space": owner})

    def pair(turn, carry):
        step = lax.rem(place * pairs // cycle + 1 + turn, pairs)
        attend(step, q_ref, k_ref, v_ref, attn_ref, pb_ref, tables, far, (0, 1, 3), False, *states)
        lanes = pl.ds(pl.multiple_of(step * LANES, LANES), LANES)
        total = lax.dot_general(
            attn_ref[:, lanes], cot_ref[...], (((0,), (0,)), ((), ())), preferred_element_type=jnp.float32
        ).astype(jnp.bfloat16)
        for part in range(per_pair):
            gsend_ref[step * per_pair + part] = total[part * grain : (part + 1) * grain]
        for part in range(per_pair):
            owner, copy = share_of(step * per_pair + part)

            @pl.when(owner != place)
            def _():
                copy.start()

        return carry

    lax.fori_loop(0, pairs, pair, 0)
    out_ref[...] = (
        hid_ref[...].reshape(patches * PATCH, features).astype(jnp.float32)
        + jnp.dot(attn_ref[...], weight_ref[7], preferred_element_type=jnp.float32)
    ).astype(jnp.bfloat16)
    sums = []
    for part in range(per_owner):
        sums.append(gsend_ref[place * per_owner + part].astype(jnp.float32))
        for k in range(cycle - 1):
            slot = k * per_owner + part
            remote(gsend_ref.at[0], grecv_ref.at[slot], share_send.at[0], share_recv.at[slot],
                   {"space": partner}).wait_recv()
            sums[-1] = sums[-1] + grecv_ref[slot].astype(jnp.float32)
    gathered = jnp.concatenate(sums, axis=0)
    piece = share // levels
    for i in range(levels):
        lsend_ref[i] = gathered[i * piece : (i + 1) * piece].astype(jnp.bfloat16)
    parts = []
    for k, peer in enumerate(peers):
        parts.append(remote(lsend_ref.at[peer], lrecv_ref.at[k], part_send.at[k], part_recv.at[k], {"level": peer}))
        parts[-1].start()
    gathered = lsend_ref[level].astype(jnp.float32)
    for k, step in enumerate(parts):
        step.wait_recv()
        gathered = gathered + lrecv_ref[k].astype(jnp.float32)
    final_ref[level] = gathered.astype(jnp.bfloat16)
    fulls = []
    for k, peer in enumerate(peers):
        fulls.append(remote(final_ref.at[level], final_ref.at[level], full_send.at[k], full_recv.at[k],
                            {"level": peer}))
        fulls[-1].start()
    for step in fulls:
        step.wait_recv()
    grad_ref[...] = final_ref[...]
    for steps in inward + back + halo + [parts, fulls]:
        for step in steps:
            step.wait_send()

    def drained(index, carry):
        owner, copy = share_of(index)

        @pl.when(owner != place)
        def _():
            copy.wait_send()

        return carry

    lax.fori_loop(0, pairs * per_pair, drained, 0)


def body(fields, norm_vert, query_vert, keys_vert, values_vert, out_vert, level_bias, norm_patch, query_patch,
         keys_patch, values_patch, out_patch, patch_bias, neighbours, counts, cotangent):
    _, tokens, features = fields.shape
    levels = lax.axis_size("level")
    cycle = lax.axis_size("space")
    patches = tokens // PATCH
    chunks = patches * SPLIT
    columns = PATCH // SPLIT // levels
    grain = math.gcd(features // cycle, LANES)
    share = features // cycle
    x = fields.reshape(chunks, levels, columns, features)
    vmem = pl.BlockSpec(memory_space=pltpu.VMEM)
    smem = pl.BlockSpec(memory_space=pltpu.SMEM)
    hbm = pl.BlockSpec(memory_space=pl.ANY)
    narrow = lambda *shape: pltpu.VMEM(shape, jnp.bfloat16)
    dma = lambda *shape: pltpu.SemaphoreType.DMA(shape)
    blocks = 5 * patches
    out, grad = pl.pallas_call(
        functools.partial(whole_kernel, cycle, levels),
        out_shape=(
            jax.ShapeDtypeStruct((tokens, features), jnp.bfloat16),
            jax.ShapeDtypeStruct((levels, share // levels, features), jnp.bfloat16),
        ),
        in_specs=[vmem] * 3 + [hbm] * 9 + [smem] * 4,
        out_specs=(vmem, vmem),
        scratch_shapes=[
            narrow(8, features, features),
            narrow(tokens, features),
            narrow(chunks, levels, columns, features),
            narrow(chunks, levels, columns, features),
            narrow(chunks, levels, columns, features),
            narrow(tokens, features),
            narrow(chunks, PATCH // SPLIT, features),
            narrow(4 * chunks, PATCH // SPLIT, features),
            narrow(tokens, features),
            narrow(blocks, PATCH, features),
            narrow(blocks, PATCH, features),
            narrow(features // grain, grain, features),
            narrow((cycle - 1) * share // grain, grain, features),
            narrow(levels, share // levels, features),
            narrow(levels - 1, share // levels, features),
            narrow(levels, share // levels, features),
            pltpu.VMEM((tokens, features), jnp.float32),
            pltpu.VMEM((tokens, features), jnp.float32),
            pltpu.VMEM((tokens, features), jnp.float32),
            dma(9),
            dma(chunks, levels - 1),
            dma(chunks, levels - 1),
            dma(chunks, levels - 1),
            dma(chunks, levels - 1),
            dma(chunks, 4),
            dma(chunks, 4),
            dma(features // grain),
            dma((cycle - 1) * share // grain),
            dma(levels - 1),
            dma(levels - 1),
            dma(levels - 1),
            dma(levels - 1),
        ],
        compiler_params=pltpu.CompilerParams(
            collective_id=0, has_side_effects=True, vmem_limit_bytes=VMEM_LIMIT
        ),
        name="whole_block",
    )(x, norm_vert, norm_patch, query_vert, keys_vert, values_vert, out_vert, query_patch, keys_patch,
      values_patch, out_patch, cotangent[0], jnp.transpose(level_bias, (1, 2, 0)), patch_bias.T, neighbours, counts)
    return (out[None], grad.astype(jnp.float32).reshape(share, features))


def solution(mesh):
    split = P("level", "space", None)
    return jax.shard_map(
        body,
        mesh=mesh,
        in_specs=(split,) + (P(),) * 12 + (P("space", None), P("space"), split),
        out_specs=(split, P("space", None)),
        check_vma=False,
    )
```
